256 devices in a mesh: rep: 32 (over x, y, core), tp: 8 (over z).
Axes of the slice: x: 4, y: 4, z: 8, core: 2. Of those that a mesh axis runs over, the one named last changes fastest.
Arguments:
- hidden_in: bfloat16 [3072, 8192], P('rep', 'tp'), may hold values from -6 to 6
- queries: bfloat16 [3072, 8192], P('rep', 'tp'), may hold values from -20 to 20
- cache_keys: bfloat16 [3072, 128, 1024], P('rep', None, 'tp'), may hold values from -6 to 6
- cached_value_rows: bfloat16 [3072, 128, 1024], P('rep', None, 'tp'), may hold values from -6 to 6
- cache_lengths: int32 [3072], P('rep'), may hold values from 1 to 128, 98304 in all
- base_key_matrix: bfloat16 [8192, 1024], P(None, 'tp'), may hold values from -0.0625 to 0.0625
- base_value_matrix: bfloat16 [8192, 1024], P(None, 'tp'), may hold values from -0.0625 to 0.0625
- shrink_weights: bfloat16 [128, 8192, 128], P('rep', 'tp'), may hold values from -0.0625 to 0.0625
- pooled_up_weights: bfloat16 [128, 2, 64, 1024], P('rep', None, None, 'tp'), may hold values from -0.75 to 0.75
- block_owner: int32 [768, 1], P('rep'), may hold values from 0 to 31; in each aligned block of 24 rows (0 to 23, 24 to 47, ...) at most 2 rows name the same one
- block_slot: int32 [768], P('rep'), may hold values from 0 to 3
Outputs:
- new_keys: bfloat16 [3072, 1024], P('rep', 'tp')
- new_values: bfloat16 [3072, 1024], P('rep', 'tp')
- context: bfloat16 [3072, 8192], P('rep', 'tp')
The draws below stay inside these ranges and needn't reach their ends.
Inputs may be any that keep to these rules, and one draw needn't show every extreme that they name: `block_owner`: among the 24 blocks of one replica group at most 2 name the same owner, and some group in every draw has 2 blocks with one owner.
All inputs are finite; a program needn't handle non-finite values. No bound on the sum of `cache_lengths` on one device may be relied on, other than what follows from the above.
Results may differ from the reference program's by a relative error of at most 0.0055.
Values may be sent and summed in bfloat16 or wider, within the bound.
A program may use at most 128 MiB of HBM per device.

```python
import math
import jax
import jax.numpy as jnp
import numpy as np
from jax import lax

MODEL_WIDTH = 8192
QUERY_HEAD_COUNT = 64
KEY_VALUE_HEADS = 8
HEAD_SIZE = 128
ADAPTER_RANK = 64
ADP_DEV = 4
ADAPTER_POOL = 128
ROWS_DEV = 96
SEQUENCE_COUNT = 3072
BLK = 4
BLOCKS = 24
CAP = 2
CONTEXT_LENGTH = 128
N_REP = 32


def draw_queries(key, part):
    drawn_result = jnp.clip(jax.random.normal(jax.random.fold_in(key, 21), (SEQUENCE_COUNT, QUERY_HEAD_COUNT * HEAD_SIZE), jnp.float32), -6.0, 6.0)
    return drawn_result.astype(jnp.bfloat16)


def draw_cache_keys(key, part):
    drawn_result = jnp.clip(jax.random.normal(jax.random.fold_in(key, 31), (SEQUENCE_COUNT, CONTEXT_LENGTH, KEY_VALUE_HEADS * HEAD_SIZE), jnp.float32), -6.0, 6.0)
    return drawn_result.astype(jnp.bfloat16)


def place_ends(drawn, key, smallest, largest):
    longest = drawn.shape.index(max(drawn.shape))
    spots = []
    for shift in (0, 1):
        where = [jax.random.randint(jax.random.fold_in(key, axis), (), 0, length) for axis, length in enumerate(drawn.shape)]
        where[longest] = (where[longest] + shift) % drawn.shape[longest]
        spots.append(tuple(where))
    return drawn.at[spots[0]].set(smallest).at[spots[1]].set(largest)


def level_of(rng, shape, cuts, low, high):
    level = 1.0
    for dim, parts in cuts:
        draws = jax.random.uniform(jax.random.fold_in(jax.random.fold_in(rng, 6), dim), (parts,), jnp.float32, low / len(cuts), high / len(cuts))
        level = level * jnp.repeat(jnp.exp(draws), shape[dim] // parts).reshape((-1,) + (1,) * (len(shape) - 1 - dim))
    return level


def profile(number_of, total, reach, slope):
    portions = [(1 << 20) // math.isqrt(standing ** slope) + 1 for standing in range(2, number_of + 1)]
    spare, counts = total - reach - (number_of - 1), [1] * (number_of - 1)
    while spare > 0:
        candidates = [i for i in range(number_of - 1) if counts[i] < reach]
        mass, budget = sum([portions[i] for i in candidates]), spare
        for i in candidates:
            more = min(reach - counts[i], max(1, budget * portions[i] // mass), spare)
            counts[i] = counts[i] + more
            spare = spare - more
    return np.array([reach] + counts)


def uneven(stream_key, number_of, total, reach, slope):
    if number_of == 2:
        one = jax.random.randint(stream_key, (), max(1, total - reach), min(reach, total - 1) + 1)
        return jnp.stack([one, total - one])
    sizes = jnp.asarray(profile(number_of, total, reach, slope), jnp.int32)
    twos = (number_of - 1) // 2
    donor, taker = sizes[1:1 + 2 * twos:2], sizes[2:2 + 2 * twos:2]
    margin = jnp.minimum(donor - 1, reach - taker)
    passed = jax.random.randint(jax.random.fold_in(stream_key, 1), (twos,), 0, 1 << 20) % (margin + 1)
    sizes = sizes.at[1:1 + 2 * twos:2].set(donor - passed).at[2:2 + 2 * twos:2].set(taker + passed)
    return sizes[jax.random.permutation(jax.random.fold_in(stream_key, 2), number_of)]


def deal_out(rng, own, number, rows, count, top, most, skew):
    sequence = jax.random.permutation(rng, count)
    packed, ordinary = shares(count, rows * top, most, skew, True), shares(count, rows * top, most, skew, False)
    places = jnp.arange(count)

    def named(sizes, turn):
        used = int((sizes > 0).sum())
        fixed = max(1, used // 4)
        shifted = fixed + (places - fixed + turn * (used - fixed)) % max(1, count - fixed)
        return jnp.zeros((count,), jnp.int32).at[sequence[jnp.where(places < fixed, places, shifted)]].set(jnp.asarray(sizes, jnp.int32))

    sizes = jnp.where(number % 4 == 0, named(packed, number // 4), named(ordinary, number - number // 4 - 1))
    mixed = jax.random.permutation(jax.random.fold_in(own, 3), count)
    donor, sink = mixed[0:count // 2 * 2:2], mixed[1:count // 2 * 2:2]
    slack = jnp.minimum(sizes[donor] - 1, most - sizes[sink]) // 2
    slack = jnp.where((donor == sequence[0]) | (sink == sequence[0]) | (sizes[sink] == 0), 0, jnp.maximum(slack, 0))
    shifted = jax.random.randint(jax.random.fold_in(own, 4), (count // 2,), 0, 1 << 20) % (slack + 1)
    sizes = sizes.at[donor].add(-shifted).at[sink].add(shifted)
    labels = jnp.searchsorted(jnp.cumsum(sizes), jnp.arange(rows * top), side="right").astype(jnp.int32)
    listing = labels.reshape(top, rows).T
    listing = listing[jax.random.permutation(jax.random.fold_in(own, 1), rows)]
    turn = jax.random.randint(jax.random.fold_in(own, 2), (rows, 1), 0, top)
    return jnp.take_along_axis(listing, (jnp.arange(top)[None, :] + turn) % top, axis=1)


def shares(count, total, most, slope, full):
    portions = [(1 << 20) // math.isqrt(standing ** slope) + 1 for standing in range(1, count + 1)]
    largest = most if full else min(most, max(-(-total // count), total * portions[0] // sum(portions)))
    least = 1 if total - largest >= count - 1 else 0
    holding, spare = [largest] + [least] * (count - 1), total - largest - least * (count - 1)
    while spare > 0:
        candidates = [i for i in range(1, count) if holding[i] < largest] or [i for i in range(1, count) if holding[i] < most]
        pool, left = sum([portions[i] for i in candidates]), spare
        for i in candidates:
            more = min(most - holding[i], max(1, left * portions[i] // pool), spare)
            holding[i] = holding[i] + more
            spare = spare - more
    return np.array(holding)


def normal_values(rng, dims, deviation, most, cuts=(), kind=jnp.bfloat16):
    entries = jax.random.normal(rng, dims, jnp.float32) * deviation
    if len(cuts) > 0:
        entries = level_of(rng, dims, cuts, -0.22, 0.18) * entries
    return jnp.clip(entries, min=-most, max=most).astype(kind)


def setup_inputs(seed: int = 0) -> dict:
    splits = jax.random.split(jax.random.key(seed), 12)
    hidden_in = normal_values(splits[0], (SEQUENCE_COUNT, MODEL_WIDTH), 1.0, 6.0, ((0, 32), (1, 8)))
    queries = draw_queries(jax.random.fold_in(splits[11], 71), 0)
    cache_keys = draw_cache_keys(jax.random.fold_in(splits[11], 71), 0)
    cached_value_rows = normal_values(splits[3], (SEQUENCE_COUNT, CONTEXT_LENGTH, KEY_VALUE_HEADS * HEAD_SIZE), 1.0, 6.0, ((0, 32), (2, 8)))
    cache_lengths = uneven(splits[4], SEQUENCE_COUNT, SEQUENCE_COUNT * CONTEXT_LENGTH // 4, CONTEXT_LENGTH, 2).astype(jnp.int32)
    base_key_matrix = normal_values(splits[5], (MODEL_WIDTH, KEY_VALUE_HEADS * HEAD_SIZE), MODEL_WIDTH ** -0.5, 0.0625, ((1, 8),))
    base_value_matrix = normal_values(splits[6], (MODEL_WIDTH, KEY_VALUE_HEADS * HEAD_SIZE), MODEL_WIDTH ** -0.5, 0.0625, ((1, 8),))
    shrink_weights = normal_values(splits[7], (ADAPTER_POOL, MODEL_WIDTH, 2 * ADAPTER_RANK), MODEL_WIDTH ** -0.5, 0.0625, ((0, 32), (1, 8)))
    pooled_up_weights = normal_values(splits[8], (ADAPTER_POOL, 2, ADAPTER_RANK, KEY_VALUE_HEADS * HEAD_SIZE), ADAPTER_RANK ** -0.5, 0.75, ((0, 32), (3, 8)))
    block_owner_keys = jax.random.split(jax.random.fold_in(splits[9], 1), (N_REP * BLOCKS) // BLOCKS)
    block_owner_turns = jax.random.permutation(jax.random.fold_in(splits[9], 3), (N_REP * BLOCKS) // BLOCKS)
    block_owner = jax.vmap(lambda own, number: deal_out(jax.random.fold_in(splits[9], 2), own, number, BLOCKS, N_REP, 1, CAP, 2))(block_owner_keys, block_owner_turns).reshape((N_REP * BLOCKS, 1))
    block_slot = place_ends(jax.random.randint(splits[10], (N_REP * BLOCKS,), 0, ADP_DEV), jax.random.fold_in(splits[10], 1), 0, ADP_DEV - 1).astype(jnp.int32)
    return dict(hidden_in=hidden_in, queries=queries, cache_keys=cache_keys, cached_value_rows=cached_value_rows, cache_lengths=cache_lengths, base_key_matrix=base_key_matrix, base_value_matrix=base_value_matrix, shrink_weights=shrink_weights, pooled_up_weights=pooled_up_weights, block_owner=block_owner, block_slot=block_slot)


adapter_scale = 0.5
masked_score = -1e30


def attend(group_queries, key_cache, value_cache, lengths, fresh_keys, fresh_values):
    rows_here = group_queries.shape[0]
    head_groups = key_cache.shape[2] // HEAD_SIZE
    group_size = group_queries.shape[1] // (head_groups * HEAD_SIZE)
    window = key_cache.shape[1]
    inverse_root = HEAD_SIZE ** -0.5
    query_heads = group_queries.reshape(rows_here, head_groups, group_size, HEAD_SIZE).astype(jnp.float32)
    key_heads = key_cache.reshape(rows_here, window, head_groups, HEAD_SIZE).astype(jnp.float32)
    value_heads = value_cache.reshape(rows_here, window, head_groups, HEAD_SIZE).astype(jnp.float32)
    scores = jnp.einsum('rkgd,rtkd->rkgt', query_heads, key_heads) * inverse_root
    own_score = jnp.einsum('rkgd,rkd->rkg', query_heads, fresh_keys.reshape(rows_here, head_groups, HEAD_SIZE).astype(jnp.float32)) * inverse_root
    visible = (jnp.arange(window, dtype=jnp.int32)[None, :] < lengths[:, None])[:, None, None, :]
    highest = jnp.maximum(jnp.max(jnp.where(visible, scores, masked_score), axis=-1), own_score)
    exp_terms = jnp.where(visible, jnp.exp(scores - highest[..., None]), 0.0)
    own_term = jnp.exp(own_score - highest)
    denominator = jnp.sum(exp_terms, axis=-1) + own_term
    weights = (exp_terms / denominator[..., None]).astype(jnp.bfloat16)
    own_weight = (own_term / denominator).astype(jnp.bfloat16)
    context = jnp.einsum('rkgt,rtkd->rkgd', weights.astype(jnp.float32), value_heads)
    context = context + own_weight.astype(jnp.float32)[..., None] * fresh_values.reshape(rows_here, head_groups, 1, HEAD_SIZE).astype(jnp.float32)
    return context.reshape(rows_here, -1).astype(jnp.bfloat16)


def reference(hidden_in, queries, cache_keys, cached_value_rows, cache_lengths, base_key_matrix, base_value_matrix, shrink_weights, pooled_up_weights, block_owner, block_slot):
    key_row_width = KEY_VALUE_HEADS * HEAD_SIZE

    def one_group(pieces):
        inputs, group_queries, group_keys, group_values, lengths, owners, slot_ids = pieces
        position = (owners[:, 0] * ADP_DEV + slot_ids).astype(jnp.int32)
        chosen_shrink = jnp.take(shrink_weights, position, axis=0).astype(jnp.float32)
        selected_expand = jnp.take(pooled_up_weights, position, axis=0).astype(jnp.float32)
        blocked = inputs.reshape(BLOCKS, BLK, MODEL_WIDTH).astype(jnp.float32)
        shrunk = jnp.einsum('bnd,bdr->bnr', blocked, chosen_shrink).astype(jnp.bfloat16)
        split_halves = shrunk.astype(jnp.float32).reshape(BLOCKS, BLK, 2, ADAPTER_RANK)
        per_row_delta = (adapter_scale * jnp.einsum('gfot,gotx->gfox', split_halves, selected_expand)).astype(jnp.bfloat16)
        per_row_delta = per_row_delta.reshape(ROWS_DEV, 2, key_row_width)
        base_keys = jnp.dot(inputs, base_key_matrix, preferred_element_type=jnp.float32)
        base_values = jnp.dot(inputs, base_value_matrix, preferred_element_type=jnp.float32)
        fresh_keys = (base_keys + per_row_delta[:, 0].astype(jnp.float32)).astype(jnp.bfloat16)
        fresh_values = (base_values + per_row_delta[:, 1].astype(jnp.float32)).astype(jnp.bfloat16)
        context = attend(group_queries, group_keys, group_values, lengths, fresh_keys, fresh_values)
        return fresh_keys, fresh_values, context

    pieces = (hidden_in.reshape(N_REP, ROWS_DEV, MODEL_WIDTH),
              queries.reshape(N_REP, ROWS_DEV, QUERY_HEAD_COUNT * HEAD_SIZE),
              cache_keys.reshape(N_REP, ROWS_DEV, CONTEXT_LENGTH, key_row_width),
              cached_value_rows.reshape(N_REP, ROWS_DEV, CONTEXT_LENGTH, key_row_width),
              cache_lengths.reshape(N_REP, ROWS_DEV),
              block_owner.reshape(N_REP, BLOCKS, 1),
              block_slot.reshape(N_REP, BLOCKS))
    fresh_keys, fresh_values, context = lax.map(one_group, pieces)
    return (fresh_keys.reshape(SEQUENCE_COUNT, key_row_width), fresh_values.reshape(SEQUENCE_COUNT, key_row_width), context.reshape(SEQUENCE_COUNT, QUERY_HEAD_COUNT * HEAD_SIZE))
```

```python
import functools
import jax
import jax.numpy as jnp
from jax import lax
from jax.experimental import pallas as pl
from jax.experimental.pallas import tpu as pltpu
from jax.sharding import PartitionSpec as P

HEAD_SIZE = 128
BLK = 4
CAP = 2
ADAPTER_SCALE = 0.5
MASKED = -1e30
MESH = pl.DeviceIdType.MESH
KV_CHUNKS = 4
UNROLL = 4


def kernel(
    N,
    T,
    lens_ref,
    owner_ref,
    slot_ref,
    hid_hbm,
    q_hbm,
    k_hbm,
    v_hbm,
    wk_hbm,
    wv_hbm,
    a_hbm,
    b_hbm,
    nk_ref,
    nv_ref,
    ctx_ref,
    hid,
    qin,
    kbuf,
    vbuf,
    wcat,
    acat,
    bcat,
    xbuf,
    sbuf,
    rbuf,
    part,
    prx,
    shr,
    srx,
    dsend,
    drx,
    qs,
    ms,
    ls,
    accs,
    base,
    load_sem,
    kv_sem,
    a2a_send,
    a2a_recv,
    ring_send,
    ring_recv,
    rs_send,
    rs_recv,
    ag_send,
    ag_recv,
    ret_send,
    ret_recv,
):
    f32, bf16 = jnp.float32, jnp.bfloat16
    R, D = hid.shape
    NB = R // BLK
    SL = CAP * BLK
    S = N * SL
    G = qin.shape[1] // HEAD_SIZE
    ADP = a_hbm.shape[0]
    RANK2 = a_hbm.shape[2]
    HALF = RANK2 // 2
    SG = S // T
    W = wk_hbm.shape[1]
    inverse_root = HEAD_SIZE ** (-0.5)
    me, z = lax.axis_index("rep"), lax.axis_index("tp")

    barrier = pltpu.get_barrier_semaphore()

    def greet_tp(i, c):
        pl.semaphore_signal(barrier, 1, device_id=(me, lax.rem(z + i, T)), device_id_type=MESH)
        return c

    def greet_rep(i, c):
        pl.semaphore_signal(barrier, 1, device_id=(lax.rem(me + i, N), z), device_id_type=MESH)
        return c

    lax.fori_loop(1, N, greet_rep, 0)
    lax.fori_loop(1, T, greet_tp, 0)

    load_hid = pltpu.make_async_copy(hid_hbm, hid, load_sem.at[0])
    load_q = pltpu.make_async_copy(q_hbm, qin, load_sem.at[1])
    load_hid.start()
    load_q.start()
    load_a = [
        pltpu.make_async_copy(
            a_hbm.at[j], acat.at[:, pl.ds(j * RANK2, RANK2)], load_sem.at[2 + j]
        )
        for j in range(ADP)
    ]
    load_w = [
        pltpu.make_async_copy(wk_hbm, wcat.at[:, pl.ds(0, W)], load_sem.at[2 + ADP]),
        pltpu.make_async_copy(wv_hbm, wcat.at[:, pl.ds(W, W)], load_sem.at[3 + ADP]),
    ]
    bcat[...] = jnp.zeros_like(bcat)
    load_b = [
        pltpu.make_async_copy(
            b_hbm.at[j, i],
            bcat.at[pl.ds(j * RANK2 + i * HALF, HALF), pl.ds(i * W, W)],
            load_sem.at[4 + ADP + 2 * j + i],
        )
        for j in range(ADP)
        for i in range(2)
    ]
    RC = R // KV_CHUNKS
    load_kv = [
        [
            pltpu.make_async_copy(
                src.at[pl.ds(c * RC, RC)], dst.at[pl.ds(c * RC, RC)], kv_sem.at[i, c]
            )
            for i, (src, dst) in enumerate(((k_hbm, kbuf), (v_hbm, vbuf)))
        ]
        for c in range(KV_CHUNKS)
    ]
    for pair in load_kv:
        for c in pair:
            c.start()
    for c in load_a:
        c.start()
    for c in load_w:
        c.start()

    lane = lax.broadcasted_iota(jnp.int32, (1, R), 1)
    block_of = lane // BLK
    owners = jnp.zeros((1, R), jnp.int32)
    slots = jnp.zeros((1, R), jnp.int32)
    for b in range(NB):
        owners = jnp.where(block_of == b, owner_ref[b], owners)
        slots = jnp.where(block_of == b, slot_ref[b], slots)
    ranks = jnp.zeros((1, R), jnp.int32)
    for b in range(NB):
        ranks = ranks + jnp.where((owners == owner_ref[b]) & (block_of > b), 1, 0)
    code = owners * SL + ranks * BLK + lane % BLK
    eye = lax.broadcasted_iota(jnp.int32, (R, R), 0) == lax.broadcasted_iota(jnp.int32, (R, R), 1)
    code_col = jnp.sum(jnp.where(eye, code.astype(f32), 0.0), axis=1, keepdims=True)
    slot_col = jnp.sum(jnp.where(eye, slots.astype(f32), 0.0), axis=1, keepdims=True)
    picks = (lax.broadcasted_iota(jnp.int32, (S, R), 0) == code).astype(bf16)
    one_hot = (
        lax.broadcasted_iota(jnp.int32, (R, 128), 1).astype(f32) == slot_col
    ).astype(bf16)
    load_hid.wait()
    sbuf[:, :, D:] = (
        jnp.dot(picks, one_hot, preferred_element_type=f32).reshape(N, SL, 128).astype(bf16)
    )
    for n in range(0, D, 256):
        sbuf[:, :, n : n + 256] = (
            jnp.dot(picks, hid[:, n : n + 256], preferred_element_type=f32)
            .reshape(N, SL, 256)
            .astype(bf16)
        )
    for c in load_b:
        c.start()

    def ring(direction, d, h, arriving):
        step = d if arriving else d - 1
        s = lax.rem(z + (T - step), T) if direction == 0 else lax.rem(z + step, T)
        to = lax.rem(z + 1, T) if direction == 0 else lax.rem(z + (T - 1), T)
        rows = pl.ds(h * (R // 2), R // 2)
        src = hid.at[rows] if d == 1 else xbuf.at[s, rows]
        return pltpu.make_async_remote_copy(
            src_ref=src,
            dst_ref=xbuf.at[s, rows],
            send_sem=ring_send.at[direction, d - 1, h],
            recv_sem=ring_recv.at[direction, d - 1, h],
            device_id=(me, to),
            device_id_type=MESH,
        )

    def carries(direction, d, h):
        return d < T // 2 or (d == T // 2 and h == direction)

    def a2a(i, arriving):
        peer = lax.rem(me + i, N)
        frm = peer if arriving else me
        return pltpu.make_async_remote_copy(
            src_ref=sbuf.at[peer],
            dst_ref=rbuf.at[frm],
            send_sem=a2a_send.at[peer],
            recv_sem=a2a_recv.at[frm],
            device_id=(peer, z),
            device_id_type=MESH,
        )

    def scatter(i, arriving):
        peer = lax.rem(z + i, T)
        frm = peer if arriving else z
        return pltpu.make_async_remote_copy(
            src_ref=part.at[peer],
            dst_ref=prx.at[frm],
            send_sem=rs_send.at[peer],
            recv_sem=rs_recv.at[frm],
            device_id=(me, peer),
            device_id_type=MESH,
        )

    def gather(i, arriving):
        peer = lax.rem(z + i, T)
        frm = peer if arriving else z
        return pltpu.make_async_remote_copy(
            src_ref=shr,
            dst_ref=srx.at[frm],
            send_sem=ag_send.at[peer],
            recv_sem=ag_recv.at[frm],
            device_id=(me, peer),
            device_id_type=MESH,
        )

    def give_back(i, arriving):
        peer = lax.rem(me + i, N)
        frm = peer if arriving else me
        return pltpu.make_async_remote_copy(
            src_ref=dsend.at[peer],
            dst_ref=drx.at[frm],
            send_sem=ret_send.at[peer],
            recv_sem=ret_recv.at[frm],
            device_id=(peer, z),
            device_id_type=MESH,
        )

    def loop(n, f):
        def step(i, c):
            f(i)
            return c

        lax.fori_loop(1, n, step, 0)

    def ring_events(d):
        for h in range(2):
            for direction in range(2):
                if carries(direction, d, h):
                    ring(direction, d, h, True).wait_recv()
                    if carries(direction, d + 1, h):
                        ring(direction, d + 1, h, False).start()

    def base_block(s, first=False):
        x = hid[...] if first else xbuf[s]
        y = jnp.dot(
            x, wcat[pl.ds(pl.multiple_of(s * D, D), D), :], preferred_element_type=f32
        )
        base[...] = y if first else base[...] + y

    def attend(chunk):
        for c in load_kv[chunk]:
            c.wait()
        position = lax.broadcasted_iota(jnp.int32, (G, k_hbm.shape[1]), 1)

        def step(i, carry):
            for u in range(UNROLL):
                r = chunk * RC + i * UNROLL + u
                q = qs[r].astype(bf16)
                s = lax.dot_general(
                    q, kbuf[r], (((1,), (1,)), ((), ())), preferred_element_type=f32
                )
                s = jnp.where(position < lens_ref[r], s * inverse_root, MASKED)
                m = jnp.max(s, axis=-1, keepdims=True)
                p = jnp.exp(s - m)
                l = jnp.sum(p, axis=-1, keepdims=True)
                accs[r] = jnp.dot(p.astype(bf16), vbuf[r], preferred_element_type=f32)
                ms[r] = jnp.broadcast_to(m, (G, HEAD_SIZE))
                ls[r] = jnp.broadcast_to(l, (G, HEAD_SIZE))
            return carry

        lax.fori_loop(0, RC // UNROLL, step, 0)

    pl.semaphore_wait(barrier, N - 1 + T - 1)
    for h in range(2):
        for direction in range(2):
            ring(direction, 1, h, False).start()
    loop(N, lambda i: a2a(i, False).start())
    rbuf[me] = sbuf[me]

    load_q.wait()
    for g in range(G):
        qs[:, g, :] = qin[:, g * HEAD_SIZE : (g + 1) * HEAD_SIZE].astype(f32)
    attend(0)
    ring_events(1)
    attend(1)
    ring_events(2)
    attend(2)
    loop(N, lambda i: a2a(i, True).wait_recv())

    for c in load_a:
        c.wait()
    rows = rbuf[...].astype(f32).reshape(S, D + 128).astype(bf16)
    y = jnp.dot(rows[:, :D], acat[...], preferred_element_type=f32)
    hot = rows[:, D:].astype(f32)
    partial = jnp.zeros((S, RANK2), f32)
    for j in range(ADP):
        partial = partial + y[:, j * RANK2 : (j + 1) * RANK2] * hot[:, j : j + 1]
    part[...] = partial.reshape(T, SG, RANK2)
    loop(T, lambda i: scatter(i, False).start())
    prx[z] = part[z]
    ring_events(3)
    for c in load_w:
        c.wait()
    base_block(z, True)
    attend(3)
    loop(T, lambda i: scatter(i, True).wait_recv())
    total = prx[0]
    for t in range(1, T):
        total = total + prx[t]
    shr[...] = total.astype(bf16)
    loop(T, lambda i: gather(i, False).start())
    srx[z] = shr[...]
    for d in range(1, T // 2):
        base_block(lax.rem(z + d, T))
        base_block(lax.rem(z + (T - d), T))
    loop(T, lambda i: gather(i, True).wait_recv())
    for c in load_b:
        c.wait()
    shrunk = srx[...].reshape(S, RANK2)
    masked = jnp.concatenate(
        [shrunk * hot[:, j : j + 1].astype(bf16) for j in range(ADP)], axis=1
    )
    delta = ADAPTER_SCALE * jnp.dot(masked, bcat[...], preferred_element_type=f32)
    dsend[...] = delta.reshape(N, SL, 2 * W).astype(bf16)
    loop(N, lambda i: give_back(i, False).start())
    drx[me] = dsend[me]
    ring_events(T // 2)
    base_block(lax.rem(z + T // 2, T))
    loop(N, lambda i: give_back(i, True).wait_recv())

    spread = (
        lax.broadcasted_iota(jnp.int32, (R, S), 1).astype(f32) == code_col
    ).astype(bf16)
    got = drx[...].astype(f32).reshape(S, 2 * W).astype(bf16)
    fresh = (base[...] + jnp.dot(spread, got, preferred_element_type=f32)).astype(bf16)
    nk_ref[...] = fresh[:, :W]
    nv_ref[...] = fresh[:, W:]
    fresh = fresh.astype(f32)
    base[...] = fresh
    nk = fresh[:, :W].reshape(R, 1, W)
    nv = fresh[:, W:].reshape(R, 1, W)
    own = jnp.sum(qs[...] * nk, axis=-1, keepdims=True) * inverse_root
    m_c = ms[...]
    top = jnp.maximum(m_c, own)
    a_c = jnp.exp(m_c - top)
    a_o = jnp.exp(own - top)
    inv = 1.0 / (ls[...] * a_c + a_o)
    w_o = (a_o * inv).astype(bf16).astype(f32)
    accs[...] = accs[...] * (a_c * inv) + w_o * nv
    for g in range(G):
        ctx_ref[:, g * HEAD_SIZE : (g + 1) * HEAD_SIZE] = accs[:, g, :].astype(bf16)

    for h in range(2):
        for direction in range(2):
            for d in range(1, T // 2 + 1):
                if carries(direction, d, h):
                    ring(direction, d, h, False).wait_send()
    loop(N, lambda i: a2a(i, False).wait_send())
    loop(T, lambda i: scatter(i, False).wait_send())
    loop(T, lambda i: gather(i, False).wait_send())
    loop(N, lambda i: give_back(i, False).wait_send())


def shards(
    hidden_in,
    queries,
    cache_keys,
    cached_value_rows,
    cache_lengths,
    base_key_matrix,
    base_value_matrix,
    shrink_weights,
    pooled_up_weights,
    block_owner,
    block_slot,
):
    N, T = lax.axis_size("rep"), lax.axis_size("tp")
    R, D = hidden_in.shape
    C = cache_keys.shape[1]
    W = base_key_matrix.shape[1]
    G = queries.shape[1] // HEAD_SIZE
    ADP, _, RANK2 = shrink_weights.shape
    SL = CAP * BLK
    S = N * SL
    f32, bf16 = jnp.float32, jnp.bfloat16
    smem = pl.BlockSpec(memory_space=pltpu.SMEM)
    hbm = pl.BlockSpec(memory_space=pl.ANY)
    vmem = pl.BlockSpec(memory_space=pltpu.VMEM)
    dma = pltpu.SemaphoreType.DMA
    return pl.pallas_call(
        functools.partial(kernel, N, T),
        out_shape=(
            jax.ShapeDtypeStruct((R, W), bf16),
            jax.ShapeDtypeStruct((R, W), bf16),
            jax.ShapeDtypeStruct((R, G * HEAD_SIZE), bf16),
        ),
        in_specs=[smem] * 3 + [hbm] * 8,
        out_specs=(vmem, vmem, vmem),
        scratch_shapes=[
            pltpu.VMEM((R, D), bf16),
            pltpu.VMEM((R, G * HEAD_SIZE), bf16),
            pltpu.VMEM((R, C, W), bf16),
            pltpu.VMEM((R, C, W), bf16),
            pltpu.VMEM((T * D, 2 * W), bf16),
            pltpu.VMEM((D, ADP * RANK2), bf16),
            pltpu.VMEM((ADP * RANK2, 2 * W), bf16),
            pltpu.VMEM((T, R, D), bf16),
            pltpu.VMEM((N, SL, D + 128), bf16),
            pltpu.VMEM((N, SL, D + 128), bf16),
            pltpu.VMEM((T, S // T, RANK2), f32),
            pltpu.VMEM((T, S // T, RANK2), f32),
            pltpu.VMEM((S // T, RANK2), bf16),
            pltpu.VMEM((T, S // T, RANK2), bf16),
            pltpu.VMEM((N, SL, 2 * W), bf16),
            pltpu.VMEM((N, SL, 2 * W), bf16),
            pltpu.VMEM((R, G, HEAD_SIZE), f32),
            pltpu.VMEM((R, G, HEAD_SIZE), f32),
            pltpu.VMEM((R, G, HEAD_SIZE), f32),
            pltpu.VMEM((R, G, HEAD_SIZE), f32),
            pltpu.VMEM((R, 2 * W), f32),
            dma((4 + 3 * ADP,)),
            dma((2, KV_CHUNKS)),
            dma((N,)),
            dma((N,)),
            dma((2, T // 2, 2)),
            dma((2, T // 2, 2)),
            dma((T,)),
            dma((T,)),
            dma((T,)),
            dma((T,)),
            dma((N,)),
            dma((N,)),
        ],
        compiler_params=pltpu.CompilerParams(
            collective_id=0, has_side_effects=True, vmem_limit_bytes=48 * 1024 * 1024
        ),
    )(
        cache_lengths,
        block_owner[:, 0],
        block_slot,
        hidden_in,
        queries,
        cache_keys,
        cached_value_rows,
        base_key_matrix,
        base_value_matrix,
        shrink_weights,
        pooled_up_weights,
    )


def solution(mesh):
    return jax.shard_map(
        shards,
        mesh=mesh,
        in_specs=(
            P("rep", "tp"),
            P("rep", "tp"),
            P("rep", None, "tp"),
            P("rep", None, "tp"),
            P("rep"),
            P(None, "tp"),
            P(None, "tp"),
            P("rep", "tp", None),
            P("rep", None, None, "tp"),
            P("rep", None),
            P("rep"),
        ),
        out_specs=(P("rep", "tp"), P("rep", "tp"), P("rep", "tp")),
        check_vma=False,
    )
```

```python
import functools
import jax
import jax.numpy as jnp
from jax import lax
from jax.experimental import pallas as pl
from jax.experimental.pallas import tpu as pltpu
from jax.sharding import PartitionSpec as P

HEAD_SIZE = 128
BLK = 4
CAP = 2
ADAPTER_SCALE = 0.5
MASKED = -1e30
MESH = pl.DeviceIdType.MESH
KV_CHUNKS = 6
EARLY = 1
VMEM_LIMIT = 40 * 1024 * 1024


def kernel(
    N,
    T,
    lens_hbm,
    owner_hbm,
    slot_hbm,
    hid_hbm,
    q_hbm,
    k_hbm,
    v_hbm,
    wk_hbm,
    wv_hbm,
    a_hbm,
    b_hbm,
    nk_ref,
    nv_ref,
    ctx_ref,
    lens_ref,
    owner_ref,
    slot_ref,
    hid,
    qin,
    kbuf,
    vbuf,
    wcat,
    acat,
    bcat,
    xbuf,
    sbuf,
    rbuf,
    part,
    prx,
    shr,
    srx,
    dsend,
    drx,
    qs,
    ms,
    ls,
    accs,
    base,
    hot,
    load_sem,
    kv_sem,
    a2a_send,
    a2a_recv,
    ring_send,
    ring_recv,
    rs_sem,
    ag_sem,
    ret_sem,
):
    f32, bf16 = jnp.float32, jnp.bfloat16
    R, D = hid.shape
    NB = R // BLK
    SL = CAP * BLK
    S = N * SL
    G = qin.shape[1] // HEAD_SIZE
    ADP = a_hbm.shape[0]
    RANK2 = a_hbm.shape[2]
    HALF = RANK2 // 2
    SG = S // T
    W = wk_hbm.shape[1]
    inverse_root = HEAD_SIZE ** (-0.5)
    me, z = lax.axis_index("rep"), lax.axis_index("tp")

    barrier = pltpu.get_barrier_semaphore()

    NC, NY = 2, 4
    NX = N // (NC * NY)
    mc, my, mx = lax.rem(me, NC), lax.rem(me // NC, NY), me // (NC * NY)
    xs = [lax.rem(mx + i, NX) * (NC * NY) for i in range(NX)]
    ys = [lax.rem(my + i, NY) * NC for i in range(NY)]
    cs = [mc, 1 - mc]
    far = lambda n: sorted(range(n), key=lambda i: -min(i, n - i))
    rep_peers = [
        xs[i] + ys[j] + cs[k]
        for i, j, k in sorted(
            ((i, j, k) for i in range(NX) for j in range(NY) for k in range(NC)),
            key=lambda t: -(min(t[0], NX - t[0]) + min(t[1], NY - t[1])),
        )
        if (i, j, k) != (0, 0, 0)
    ]
    tp_peers = [lax.rem(z + i, T) for i in far(T) if i]
    load_hid = pltpu.make_async_copy(hid_hbm, hid, load_sem.at[0])
    load_q = pltpu.make_async_copy(q_hbm, qin, load_sem.at[1])
    load_ids = [
        pltpu.make_async_copy(owner_hbm, owner_ref, load_sem.at[4 + 3 * ADP]),
        pltpu.make_async_copy(slot_hbm, slot_ref, load_sem.at[5 + 3 * ADP]),
        pltpu.make_async_copy(lens_hbm, lens_ref, load_sem.at[6 + 3 * ADP]),
    ]
    load_hid.start()
    for c in load_ids:
        c.start()
    load_q.start()
    for p in tp_peers:
        pl.semaphore_signal(barrier, 1, device_id=(me, p), device_id_type=MESH)
    for p in rep_peers:
        pl.semaphore_signal(barrier, 1, device_id=(p, z), device_id_type=MESH)
    load_a = [
        pltpu.make_async_copy(
            a_hbm.at[j], acat.at[:, pl.ds(j * RANK2, RANK2)], load_sem.at[2 + j]
        )
        for j in range(ADP)
    ]
    load_w = [
        pltpu.make_async_copy(wk_hbm, wcat.at[:, pl.ds(0, W)], load_sem.at[2 + ADP]),
        pltpu.make_async_copy(wv_hbm, wcat.at[:, pl.ds(W, W)], load_sem.at[3 + ADP]),
    ]
    bcat[...] = jnp.zeros_like(bcat)
    load_b = [
        pltpu.make_async_copy(
            b_hbm.at[j, i],
            bcat.at[pl.ds(j * RANK2 + i * HALF, HALF), pl.ds(i * W, W)],
            load_sem.at[4 + ADP + 2 * j + i],
        )
        for j in range(ADP)
        for i in range(2)
    ]
    RC = R // KV_CHUNKS
    load_kv = [
        [
            pltpu.make_async_copy(
                src.at[pl.ds(c * RC, RC)], dst.at[pl.ds(c * RC, RC)], kv_sem.at[i, c]
            )
            for i, (src, dst) in enumerate(((k_hbm, kbuf), (v_hbm, vbuf)))
        ]
        for c in range(KV_CHUNKS)
    ]
    for pair in load_kv:
        for c in pair:
            c.start()
    for c in load_a:
        c.start()
    for c in load_w:
        c.start()

    lane = lax.broadcasted_iota(jnp.int32, (1, R), 1)
    block_of = lane // BLK
    for c in load_ids:
        c.wait()
    owners = jnp.zeros((1, R), jnp.int32)
    slots = jnp.zeros((1, R), jnp.int32)
    for b in range(NB):
        owners = jnp.where(block_of == b, owner_ref[b], owners)
        slots = jnp.where(block_of == b, slot_ref[b], slots)
    ranks = jnp.zeros((1, R), jnp.int32)
    for b in range(NB):
        ranks = ranks + jnp.where((owners == owner_ref[b]) & (block_of > b), 1, 0)
    code = owners * SL + ranks * BLK + lane % BLK
    eye = lax.broadcasted_iota(jnp.int32, (R, R), 0) == lax.broadcasted_iota(jnp.int32, (R, R), 1)
    code_col = jnp.sum(jnp.where(eye, code.astype(f32), 0.0), axis=1, keepdims=True)
    slot_col = jnp.sum(jnp.where(eye, slots.astype(f32), 0.0), axis=1, keepdims=True)
    picks = (lax.broadcasted_iota(jnp.int32, (S, R), 0) == code).astype(bf16)
    one_hot = (
        lax.broadcasted_iota(jnp.int32, (R, 128), 1).astype(f32) == slot_col
    ).astype(bf16)
    load_hid.wait()
    sbuf[:, :, D:] = (
        jnp.dot(picks, one_hot, preferred_element_type=f32).reshape(N, SL, 128).astype(bf16)
    )
    for n in range(0, D, 256):
        sbuf[:, :, n : n + 256] = (
            jnp.dot(picks, hid[:, n : n + 256], preferred_element_type=f32)
            .reshape(N, SL, 256)
            .astype(bf16)
        )
    for c in load_b:
        c.start()

    def ring(direction, d, h, arriving):
        step = d if arriving else d - 1
        s = lax.rem(z + (T - step), T) if direction == 0 else lax.rem(z + step, T)
        to = lax.rem(z + 1, T) if direction == 0 else lax.rem(z + (T - 1), T)
        rows = pl.ds(h * (R // 2), R // 2)
        src = hid.at[rows] if d == 1 else xbuf.at[s, rows]
        return pltpu.make_async_remote_copy(
            src_ref=src,
            dst_ref=xbuf.at[s, rows],
            send_sem=ring_send.at[direction, d - 1, h],
            recv_sem=ring_recv.at[direction, d - 1, h],
            device_id=(me, to),
            device_id_type=MESH,
        )

    def carries(direction, d, h):
        return d < T // 2 or (d == T // 2 and h == direction)

    def to_rep(src, dst, sems, peer):
        return pltpu.make_async_remote_copy(
            src_ref=src,
            dst_ref=dst,
            send_sem=sems.at[0],
            recv_sem=sems.at[1],
            device_id=(peer, z),
            device_id_type=MESH,
        )

    def to_tp(src, dst, sems, peer):
        return pltpu.make_async_remote_copy(
            src_ref=src,
            dst_ref=dst,
            send_sem=sems.at[0],
            recv_sem=sems.at[1],
            device_id=(me, peer),
            device_id_type=MESH,
        )

    def arrived(buf, sems):
        pltpu.make_async_copy(buf, buf, sems.at[1]).wait()

    def sent(buf, sems):
        part_of = buf.at[pl.ds(0, buf.shape[0] - 1)]
        pltpu.make_async_copy(part_of, part_of, sems.at[0]).wait()

    def ring_event(d, h):
        for direction in range(2):
            if carries(direction, d, h):
                ring(direction, d, h, True).wait_recv()
                if carries(direction, d + 1, h):
                    ring(direction, d + 1, h, False).start()

    def base_block(s, first=False):
        x = hid[...] if first else xbuf[s]
        y = jnp.dot(
            x, wcat[pl.ds(pl.multiple_of(s * D, D), D), :], preferred_element_type=f32
        )
        base[...] = y if first else base[...] + y

    def attend(chunk):
        for c in load_kv[chunk]:
            c.wait()
        C = k_hbm.shape[1]
        rs = pl.ds(chunk * RC, RC)
        position = lax.broadcasted_iota(jnp.int32, (RC, G, C), 2)
        upto = jnp.stack(
            [jnp.full((G, C), lens_ref[chunk * RC + u], jnp.int32) for u in range(RC)]
        )
        s = lax.dot_general(
            qs[rs].astype(bf16),
            kbuf[rs],
            (((2,), (2,)), ((0,), (0,))),
            preferred_element_type=f32,
        )
        s = jnp.where(position < upto, s * inverse_root, MASKED)
        m = jnp.max(s, axis=-1, keepdims=True)
        p = jnp.exp(s - m)
        l = jnp.sum(p, axis=-1, keepdims=True)
        accs[rs] = lax.dot_general(
            p.astype(bf16),
            vbuf[rs],
            (((2,), (1,)), ((0,), (0,))),
            preferred_element_type=f32,
        )
        ms[rs] = jnp.broadcast_to(m, (RC, G, HEAD_SIZE))
        ls[rs] = jnp.broadcast_to(l, (RC, G, HEAD_SIZE))

    def forward_queries():
        load_q.wait()
        for g in range(G):
            qs[:, g, :] = qin[:, g * HEAD_SIZE : (g + 1) * HEAD_SIZE].astype(f32)

    forward_queries()
    for chunk in range(EARLY):
        attend(chunk)
    pl.semaphore_wait(barrier, N - 1 + T - 1)
    for h in range(2):
        for direction in range(2):
            ring(direction, 1, h, False).start()
    for i in (2, 1, 3, 0):
        for j in (2, 1, 3, 0):
            for k in (1, 0):
                p = xs[i] + ys[j] + cs[k]
                if (i, j, k) == (0, 0, 0):
                    pltpu.make_async_copy(sbuf.at[p], rbuf.at[p], a2a_recv.at[0]).start()
                else:
                    pltpu.make_async_remote_copy(
                        src_ref=sbuf.at[p],
                        dst_ref=rbuf.at[me],
                        send_sem=a2a_send,
                        recv_sem=a2a_recv.at[i],
                        device_id=(p, z),
                        device_id_type=MESH,
                    ).start()
    for chunk in range(EARLY, KV_CHUNKS):
        attend(chunk)
    for c in load_w:
        c.wait()
    base_block(z, True)
    ring_event(1, 0)
    ring_event(1, 1)

    for c in load_a:
        c.wait()
    NG = N // NX
    for i in (0, 3, 1, 2):
        x = lax.rem(mx + (NX - i), NX)
        slabs = rbuf.at[pl.ds(x * NG, NG)]
        pltpu.make_async_copy(slabs, slabs, a2a_recv.at[i]).wait()
        rows = slabs[...].astype(f32).reshape(NG * SL, D + 128)
        hot[pl.ds(x * NG * SL, NG * SL), :] = rows[:, D:]
        y = jnp.dot(rows[:, :D].astype(bf16), acat[...], preferred_element_type=f32)
        partial = jnp.zeros((NG * SL, RANK2), f32)
        for j in range(ADP):
            partial = partial + y[:, j * RANK2 : (j + 1) * RANK2] * rows[:, D + j : D + j + 1]
        TG = T // NX
        part[pl.ds(x * TG, TG)] = partial.reshape(TG, SG, RANK2).astype(part.dtype)
        for t in range(TG):
            to = x * TG + t

            @pl.when(to != z)
            def _():
                to_tp(part.at[to], prx.at[z], rs_sem, to).start()

            @pl.when(to == z)
            def _():
                pltpu.make_async_copy(part.at[to], prx.at[to], rs_sem.at[1]).start()

    ring_event(2, 0)
    base_block(lax.rem(z + 1, T))
    base_block(lax.rem(z + T - 1, T))
    arrived(prx, rs_sem)
    total = prx[0].astype(f32)
    for t in range(1, T):
        total = total + prx[t].astype(f32)
    shr[...] = total.astype(bf16)
    for p in tp_peers:
        to_tp(shr, srx.at[z], ag_sem, p).start()
    pltpu.make_async_copy(shr, srx.at[z], ag_sem.at[1]).start()
    ring_event(2, 1)
    base_block(lax.rem(z + 2, T))
    base_block(lax.rem(z + T - 2, T))
    ring_event(3, 0)
    slabs = sbuf.at[pl.ds(0, N - 1)]
    pltpu.make_async_copy(slabs, slabs, a2a_send).wait()
    sent(part, rs_sem)
    arrived(srx, ag_sem)
    for c in load_b:
        c.wait()
    shrunk = srx[...].reshape(S, RANK2)
    masked = jnp.concatenate(
        [shrunk * hot[:, j : j + 1].astype(bf16) for j in range(ADP)], axis=1
    )
    delta = ADAPTER_SCALE * jnp.dot(masked, bcat[...], preferred_element_type=f32)
    dsend[...] = delta.reshape(N, SL, 2 * W).astype(bf16)
    for p in rep_peers:
        to_rep(dsend.at[p], drx.at[me], ret_sem, p).start()
    pltpu.make_async_copy(dsend.at[me], drx.at[me], ret_sem.at[1]).start()
    ring_event(3, 1)
    base_block(lax.rem(z + 3, T))
    base_block(lax.rem(z + T - 3, T))
    for h in range(2):
        ring_event(T // 2, h)
    base_block(lax.rem(z + T // 2, T))
    for h in range(2):
        for direction in range(2):
            for d in range(1, T // 2 + 1):
                if carries(direction, d, h):
                    ring(direction, d, h, False).wait_send()
    sent(srx, ag_sem)
    arrived(drx, ret_sem)

    spread = (
        lax.broadcasted_iota(jnp.int32, (R, S), 1).astype(f32) == code_col
    ).astype(bf16)
    got = drx[...].astype(f32).reshape(S, 2 * W).astype(bf16)
    fresh = (base[...] + jnp.dot(spread, got, preferred_element_type=f32)).astype(bf16)
    nk_ref[...] = fresh[:, :W]
    nv_ref[...] = fresh[:, W:]
    fresh = fresh.astype(f32)
    base[...] = fresh
    nk = fresh[:, :W].reshape(R, 1, W)
    nv = fresh[:, W:].reshape(R, 1, W)
    own = jnp.sum(qs[...] * nk, axis=-1, keepdims=True) * inverse_root
    m_c = ms[...]
    top = jnp.maximum(m_c, own)
    a_c = jnp.exp(m_c - top)
    a_o = jnp.exp(own - top)
    inv = 1.0 / (ls[...] * a_c + a_o)
    w_o = (a_o * inv).astype(bf16).astype(f32)
    accs[...] = accs[...] * (a_c * inv) + w_o * nv
    for g in range(G):
        ctx_ref[:, g * HEAD_SIZE : (g + 1) * HEAD_SIZE] = accs[:, g, :].astype(bf16)

    sent(dsend, ret_sem)


def put_out(a_ref, b_ref, c_ref, a_out, b_out, c_out, sem):
    copies = [
        pltpu.make_async_copy(src, dst, sem.at[i])
        for i, (src, dst) in enumerate(((c_ref, c_out), (a_ref, a_out), (b_ref, b_out)))
    ]
    for c in copies:
        c.start()
    for c in copies:
        c.wait()


def shards(
    hidden_in,
    queries,
    cache_keys,
    cached_value_rows,
    cache_lengths,
    base_key_matrix,
    base_value_matrix,
    shrink_weights,
    pooled_up_weights,
    block_owner,
    block_slot,
):
    N, T = lax.axis_size("rep"), lax.axis_size("tp")
    R, D = hidden_in.shape
    C = cache_keys.shape[1]
    W = base_key_matrix.shape[1]
    G = queries.shape[1] // HEAD_SIZE
    ADP, _, RANK2 = shrink_weights.shape
    SL = CAP * BLK
    S = N * SL
    f32, bf16 = jnp.float32, jnp.bfloat16
    hbm = pl.BlockSpec(memory_space=pltpu.HBM)
    vmem = pl.BlockSpec(memory_space=pltpu.VMEM)
    dma = pltpu.SemaphoreType.DMA
    held = pl.pallas_call(
        functools.partial(kernel, N, T),
        out_shape=(
            jax.ShapeDtypeStruct((R, W), bf16),
            jax.ShapeDtypeStruct((R, W), bf16),
            jax.ShapeDtypeStruct((R, G * HEAD_SIZE), bf16),
        ),
        in_specs=[hbm] * 11,
        out_specs=(vmem, vmem, vmem),
        scratch_shapes=[
            pltpu.SMEM((R,), jnp.int32),
            pltpu.SMEM((R // BLK,), jnp.int32),
            pltpu.SMEM((R // BLK,), jnp.int32),
            pltpu.VMEM((R, D), bf16),
            pltpu.VMEM((R, G * HEAD_SIZE), bf16),
            pltpu.VMEM((R, C, W), bf16),
            pltpu.VMEM((R, C, W), bf16),
            pltpu.VMEM((T * D, 2 * W), bf16),
            pltpu.VMEM((D, ADP * RANK2), bf16),
            pltpu.VMEM((ADP * RANK2, 2 * W), bf16),
            pltpu.VMEM((T, R, D), bf16),
            pltpu.VMEM((N, SL, D + 128), bf16),
            pltpu.VMEM((N, SL, D + 128), bf16),
            pltpu.VMEM((T, S // T, RANK2), bf16),
            pltpu.VMEM((T, S // T, RANK2), bf16),
            pltpu.VMEM((S // T, RANK2), bf16),
            pltpu.VMEM((T, S // T, RANK2), bf16),
            pltpu.VMEM((N, SL, 2 * W), bf16),
            pltpu.VMEM((N, SL, 2 * W), bf16),
            pltpu.VMEM((R, G, HEAD_SIZE), f32),
            pltpu.VMEM((R, G, HEAD_SIZE), f32),
            pltpu.VMEM((R, G, HEAD_SIZE), f32),
            pltpu.VMEM((R, G, HEAD_SIZE), f32),
            pltpu.VMEM((R, 2 * W), f32),
            pltpu.VMEM((S, 128), f32),
            dma((7 + 3 * ADP,)),
            dma((2, KV_CHUNKS)),
            dma(()),
            dma((4,)),
            dma((2, T // 2, 2)),
            dma((2, T // 2, 2)),
            dma((2,)),
            dma((2,)),
            dma((2,)),
        ],
        compiler_params=pltpu.CompilerParams(
            collective_id=0, has_side_effects=True, vmem_limit_bytes=VMEM_LIMIT
        ),
    )(
        *(
            pltpu.with_memory_space_constraint(x, pltpu.HBM)
            for x in (
                cache_lengths,
                block_owner[:, 0],
                block_slot,
                hidden_in,
                queries,
                cache_keys,
                cached_value_rows,
                base_key_matrix,
                base_value_matrix,
                shrink_weights,
                pooled_up_weights,
            )
        )
    )
    return pl.pallas_call(
        put_out,
        out_shape=tuple(jax.ShapeDtypeStruct(h.shape, h.dtype) for h in held),
        in_specs=[vmem] * 3,
        out_specs=(pl.BlockSpec(memory_space=pltpu.HBM),) * 3,
        scratch_shapes=[dma((3,))],
        compiler_params=pltpu.CompilerParams(vmem_limit_bytes=1024 * 1024),
    )(*held)


def solution(mesh):
    return jax.shard_map(
        shards,
        mesh=mesh,
        in_specs=(
            P("rep", "tp"),
            P("rep", "tp"),
            P("rep", None, "tp"),
            P("rep", None, "tp"),
            P("rep"),
            P(None, "tp"),
            P(None, "tp"),
            P("rep", "tp", None),
            P("rep", None, None, "tp"),
            P("rep", None),
            P("rep"),
        ),
        out_specs=(P("rep", "tp"), P("rep", "tp"), P("rep", "tp")),
        check_vma=False,
    )
```

```python
import functools
import jax
import jax.numpy as jnp
from jax import lax
from jax.experimental import pallas as pl
from jax.experimental.pallas import tpu as pltpu
from jax.sharding import PartitionSpec as P

HEAD_SIZE = 128
BLK = 4
CAP = 2
ADAPTER_SCALE = 0.5
MASKED = -1e30
MESH = pl.DeviceIdType.MESH
KV_CHUNKS = 6
VMEM_LIMIT = 40 * 1024 * 1024


def kernel(
    N,
    T,
    lens_hbm,
    owner_hbm,
    slot_hbm,
    hid_hbm,
    q_hbm,
    k_hbm,
    v_hbm,
    wk_hbm,
    wv_hbm,
    a_hbm,
    b_hbm,
    nk_ref,
    nv_ref,
    ctx_ref,
    lens_ref,
    owner_ref,
    slot_ref,
    hid,
    qin,
    kbuf,
    vbuf,
    wcat,
    acat,
    bcat,
    xbuf,
    sbuf,
    rbuf,
    part,
    prx,
    shr,
    srx,
    dsend,
    drx,
    qs,
    ms,
    ls,
    accs,
    base,
    hot,
    acc_g,
    m_g,
    l_g,
    load_sem,
    kv_sem,
    a2a_send,
    a2a_recv,
    ring_send,
    ring_recv,
    rs_sem,
    ag_send,
    ag_recv,
    ret_sem,
):
    f32, bf16 = jnp.float32, jnp.bfloat16
    R, D = hid.shape
    NB = R // BLK
    SL = CAP * BLK
    S = N * SL
    G = qin.shape[1] // HEAD_SIZE
    ADP = a_hbm.shape[0]
    RANK2 = a_hbm.shape[2]
    HALF = RANK2 // 2
    SG = S // T
    W = wk_hbm.shape[1]
    inverse_root = HEAD_SIZE ** (-0.5)
    me, z = lax.axis_index("rep"), lax.axis_index("tp")

    barrier = pltpu.get_barrier_semaphore()

    NC, NY = 2, 4
    NX = N // (NC * NY)
    mc, my, mx = lax.rem(me, NC), lax.rem(me // NC, NY), me // (NC * NY)
    xs = [lax.rem(mx + i, NX) * (NC * NY) for i in range(NX)]
    ys = [lax.rem(my + i, NY) * NC for i in range(NY)]
    cs = [mc, 1 - mc]
    far = lambda n: sorted(range(n), key=lambda i: -min(i, n - i))
    rep_peers = [
        xs[i] + ys[j] + cs[k]
        for i, j, k in sorted(
            ((i, j, k) for i in range(NX) for j in range(NY) for k in range(NC)),
            key=lambda t: -(min(t[0], NX - t[0]) + min(t[1], NY - t[1])),
        )
        if (i, j, k) != (0, 0, 0)
    ]
    tp_peers = [lax.rem(z + i, T) for i in far(T) if i]
    for p in tp_peers:
        pl.semaphore_signal(barrier, 1, device_id=(me, p), device_id_type=MESH)
    for p in rep_peers:
        pl.semaphore_signal(barrier, 1, device_id=(p, z), device_id_type=MESH)
    load_hid = pltpu.make_async_copy(hid_hbm, hid, load_sem.at[0])
    load_q = pltpu.make_async_copy(q_hbm, qin, load_sem.at[1])
    load_ids = [
        pltpu.make_async_copy(owner_hbm, owner_ref, load_sem.at[4 + 3 * ADP]),
        pltpu.make_async_copy(slot_hbm, slot_ref, load_sem.at[5 + 3 * ADP]),
        pltpu.make_async_copy(lens_hbm, lens_ref, load_sem.at[6 + 3 * ADP]),
    ]
    load_hid.start()
    for c in load_ids:
        c.start()
    load_q.start()
    load_a = [
        pltpu.make_async_copy(
            a_hbm.at[j], acat.at[:, pl.ds(j * RANK2, RANK2)], load_sem.at[2 + j]
        )
        for j in range(ADP)
    ]
    load_w = [
        pltpu.make_async_copy(wk_hbm, wcat.at[:, pl.ds(0, W)], load_sem.at[2 + ADP]),
        pltpu.make_async_copy(wv_hbm, wcat.at[:, pl.ds(W, W)], load_sem.at[3 + ADP]),
    ]
    bcat[...] = jnp.zeros_like(bcat)
    load_b = [
        pltpu.make_async_copy(
            b_hbm.at[j, i],
            bcat.at[pl.ds(j * RANK2 + i * HALF, HALF), pl.ds(i * W, W)],
            load_sem.at[4 + ADP + 2 * j + i],
        )
        for j in range(ADP)
        for i in range(2)
    ]
    RC = R // KV_CHUNKS
    load_kv = [
        [
            pltpu.make_async_copy(
                src.at[pl.ds(c * RC, RC)], dst.at[pl.ds(c * RC, RC)], kv_sem.at[i, c]
            )
            for i, (src, dst) in enumerate(((k_hbm, kbuf), (v_hbm, vbuf)))
        ]
        for c in range(KV_CHUNKS)
    ]
    for pair in load_kv:
        for c in pair:
            c.start()
    for c in load_a:
        c.start()
    for c in load_w:
        c.start()

    lane = lax.broadcasted_iota(jnp.int32, (1, R), 1)
    block_of = lane // BLK
    for c in load_ids:
        c.wait()
    owners = jnp.zeros((1, R), jnp.int32)
    slots = jnp.zeros((1, R), jnp.int32)
    for b in range(NB):
        owners = jnp.where(block_of == b, owner_ref[b], owners)
        slots = jnp.where(block_of == b, slot_ref[b], slots)
    ranks = jnp.zeros((1, R), jnp.int32)
    for b in range(NB):
        ranks = ranks + jnp.where((owners == owner_ref[b]) & (block_of > b), 1, 0)
    code = owners * SL + ranks * BLK + lane % BLK
    eye = lax.broadcasted_iota(jnp.int32, (R, R), 0) == lax.broadcasted_iota(jnp.int32, (R, R), 1)
    code_col = jnp.sum(jnp.where(eye, code.astype(f32), 0.0), axis=1, keepdims=True)
    slot_col = jnp.sum(jnp.where(eye, slots.astype(f32), 0.0), axis=1, keepdims=True)
    picks = (lax.broadcasted_iota(jnp.int32, (S, R), 0) == code).astype(bf16)
    one_hot = (
        lax.broadcasted_iota(jnp.int32, (R, 128), 1).astype(f32) == slot_col
    ).astype(bf16)
    load_hid.wait()
    sbuf[:, :, D:] = (
        jnp.dot(picks, one_hot, preferred_element_type=f32).reshape(N, SL, 128).astype(bf16)
    )
    for n in range(0, D, 256):
        sbuf[:, :, n : n + 256] = (
            jnp.dot(picks, hid[:, n : n + 256], preferred_element_type=f32)
            .reshape(N, SL, 256)
            .astype(bf16)
        )
    for c in load_b:
        c.start()

    def ring(direction, d, h, arriving):
        step = d if arriving else d - 1
        s = lax.rem(z + (T - step), T) if direction == 0 else lax.rem(z + step, T)
        to = lax.rem(z + 1, T) if direction == 0 else lax.rem(z + (T - 1), T)
        rows = pl.ds(h * (R // 2), R // 2)
        src = hid.at[rows] if d == 1 else xbuf.at[s, rows]
        return pltpu.make_async_remote_copy(
            src_ref=src,
            dst_ref=xbuf.at[s, rows],
            send_sem=ring_send.at[direction, d - 1, h],
            recv_sem=ring_recv.at[direction, d - 1, h],
            device_id=(me, to),
            device_id_type=MESH,
        )

    def carries(direction, d, h):
        return d < T // 2 or (d == T // 2 and h == direction)

    def to_rep(src, dst, sems, peer):
        return pltpu.make_async_remote_copy(
            src_ref=src,
            dst_ref=dst,
            send_sem=sems.at[0],
            recv_sem=sems.at[1],
            device_id=(peer, z),
            device_id_type=MESH,
        )

    def to_tp(src, dst, sems, peer):
        return pltpu.make_async_remote_copy(
            src_ref=src,
            dst_ref=dst,
            send_sem=sems.at[0],
            recv_sem=sems.at[1],
            device_id=(me, peer),
            device_id_type=MESH,
        )

    def arrived(buf, sems):
        pltpu.make_async_copy(buf, buf, sems.at[1]).wait()

    def sent(buf, sems):
        part_of = buf.at[pl.ds(0, buf.shape[0] - 1)]
        pltpu.make_async_copy(part_of, part_of, sems.at[0]).wait()

    def ring_event(d, h):
        for direction in range(2):
            if carries(direction, d, h):
                ring(direction, d, h, True).wait_recv()
                if carries(direction, d + 1, h):
                    ring(direction, d + 1, h, False).start()

    def base_block(s, first=False):
        x = hid[...] if first else xbuf[s]
        y = jnp.dot(
            x, wcat[pl.ds(pl.multiple_of(s * D, D), D), :], preferred_element_type=f32
        )
        base[...] = y if first else base[...] + y

    def attend(chunk):
        for c in load_kv[chunk]:
            c.wait()
        C = k_hbm.shape[1]
        rs = pl.ds(chunk * RC, RC)
        position = lax.broadcasted_iota(jnp.int32, (RC, G, C), 2)
        upto = jnp.stack(
            [jnp.full((G, C), lens_ref[chunk * RC + u], jnp.int32) for u in range(RC)]
        )
        s = lax.dot_general(
            qs[rs].astype(bf16),
            kbuf[rs],
            (((2,), (2,)), ((0,), (0,))),
            preferred_element_type=f32,
        )
        s = jnp.where(position < upto, s * inverse_root, MASKED)
        m = jnp.max(s, axis=-1, keepdims=True)
        p = jnp.exp(s - m)
        l = jnp.sum(p, axis=-1, keepdims=True)
        accs[rs] = lax.dot_general(
            p.astype(bf16),
            vbuf[rs],
            (((2,), (1,)), ((0,), (0,))),
            preferred_element_type=f32,
        )
        ms[rs] = jnp.broadcast_to(m, (RC, G, HEAD_SIZE))
        ls[rs] = jnp.broadcast_to(l, (RC, G, HEAD_SIZE))

    def forward_queries():
        load_q.wait()
        for g in range(G):
            qs[:, g, :] = qin[:, g * HEAD_SIZE : (g + 1) * HEAD_SIZE].astype(f32)

    pl.semaphore_wait(barrier, N - 1 + T - 1)
    for h in range(2):
        for direction in range(2):
            ring(direction, 1, h, False).start()
    for i in (0, 2, 1, 3):
        for j in (2, 1, 3, 0):
            for k in (1, 0):
                p = xs[i] + ys[j] + cs[k]
                if (i, j, k) == (0, 0, 0):
                    pltpu.make_async_copy(sbuf.at[p], rbuf.at[p], a2a_recv.at[0]).start()
                else:
                    pltpu.make_async_remote_copy(
                        src_ref=sbuf.at[p],
                        dst_ref=rbuf.at[me],
                        send_sem=a2a_send,
                        recv_sem=a2a_recv.at[i],
                        device_id=(p, z),
                        device_id_type=MESH,
                    ).start()
    forward_queries()
    for chunk in range(KV_CHUNKS):
        attend(chunk)
    for c in load_w:
        c.wait()
    base_block(z, True)
    for c in load_a:
        c.wait()
    NG = N // NX
    GR = NG * SL
    TG = T // NX
    odd = lax.rem(mx, 2)
    groups = [0, 2, 1 + 2 * odd, 3 - 2 * odd]

    def sender_x(i):
        return lax.rem(mx + (NX - i), NX)

    def shrink(i):
        x = sender_x(i)
        slabs = rbuf.at[pl.ds(x * NG, NG)]
        pltpu.make_async_copy(slabs, slabs, a2a_recv.at[i]).wait()
        rows = slabs[...].astype(f32).reshape(GR, D + 128)
        hot[x] = rows[:, D:]
        y = jnp.dot(rows[:, :D].astype(bf16), acat[...], preferred_element_type=f32)
        partial = jnp.zeros((GR, RANK2), f32)
        for j in range(ADP):
            partial = partial + y[:, j * RANK2 : (j + 1) * RANK2] * rows[:, D + j : D + j + 1]
        part[pl.ds(x * TG, TG)] = partial.reshape(TG, SG, RANK2).astype(part.dtype)
        for t in range(TG):
            to = x * TG + t

            @pl.when(to != z)
            def _():
                to_tp(part.at[to], prx.at[z], rs_sem, to).start()

            @pl.when(to == z)
            def _():
                pltpu.make_async_copy(part.at[to], prx.at[to], rs_sem.at[1]).start()

    def expand(i):
        x = sender_x(i)
        slabs = srx.at[pl.ds(x * TG, TG)]
        pltpu.make_async_copy(slabs, slabs, ag_recv.at[i]).wait()
        shrunk = slabs[...].reshape(GR, RANK2)
        hots = hot[x]
        masked = jnp.concatenate(
            [shrunk * hots[:, j : j + 1].astype(bf16) for j in range(ADP)], axis=1
        )
        delta = ADAPTER_SCALE * jnp.dot(masked, bcat[...], preferred_element_type=f32)
        dsend[pl.ds(x * NG, NG)] = delta.reshape(NG, SL, 2 * W).astype(bf16)
        for j in (2, 1, 3, 0):
            for k in (1, 0):
                p = x * NG + ys[j] + cs[k]
                if not isinstance(i, int) or i != 0 or (j, k) != (0, 0):
                    to_rep(dsend.at[p], drx.at[me], ret_sem, p).start()
                else:
                    pltpu.make_async_copy(dsend.at[p], drx.at[p], ret_sem.at[1]).start()

    ring_event(1, 0)
    ring_event(1, 1)
    shrink(groups[0])
    shrink(groups[1])
    shrink(groups[2])
    shrink(groups[3])
    ring_event(2, 0)
    base_block(lax.rem(z + 1, T))
    base_block(lax.rem(z + T - 1, T))
    for src, dst in ((accs, acc_g), (ms, m_g), (ls, l_g)):
        for g in range(G):
            dst[g] = src[:, g, :]
    arrived(prx, rs_sem)
    total = prx[0].astype(f32)
    for t in range(1, T):
        total = total + prx[t].astype(f32)
    shr[...] = total.astype(bf16)
    mine = lax.rem(mx + (NX - z // TG), NX)
    for p in tp_peers:
        pltpu.make_async_remote_copy(
            src_ref=shr,
            dst_ref=srx.at[z],
            send_sem=ag_send,
            recv_sem=ag_recv.at[mine],
            device_id=(me, p),
            device_id_type=MESH,
        ).start()
    pltpu.make_async_copy(shr, srx.at[z], ag_recv.at[mine]).start()
    ring_event(2, 1)
    base_block(lax.rem(z + 2, T))
    base_block(lax.rem(z + T - 2, T))
    for c in load_b:
        c.wait()
    ring_event(3, 0)
    expand(groups[0])
    expand(groups[1])
    expand(groups[2])
    expand(groups[3])
    ring_event(3, 1)
    base_block(lax.rem(z + 3, T))
    base_block(lax.rem(z + T - 3, T))
    slabs = sbuf.at[pl.ds(0, N - 1)]
    pltpu.make_async_copy(slabs, slabs, a2a_send).wait()
    sent(part, rs_sem)
    slabs = srx.at[pl.ds(0, T - 1)]
    pltpu.make_async_copy(slabs, slabs, ag_send).wait()
    for h in range(2):
        ring_event(T // 2, h)
    base_block(lax.rem(z + T // 2, T))
    for h in range(2):
        for direction in range(2):
            for d in range(1, T // 2 + 1):
                if carries(direction, d, h):
                    ring(direction, d, h, False).wait_send()
    arrived(drx, ret_sem)

    spread = (
        lax.broadcasted_iota(jnp.int32, (R, S), 1).astype(f32) == code_col
    ).astype(bf16)
    got = drx[...].astype(f32).reshape(S, 2 * W).astype(bf16)
    fresh = (base[...] + jnp.dot(spread, got, preferred_element_type=f32)).astype(bf16)
    nk_ref[...] = fresh[:, :W]
    nv_ref[...] = fresh[:, W:]
    nk = fresh[:, :W].astype(f32)
    nv = fresh[:, W:].astype(f32)
    for g in range(G):
        q = qin[:, g * HEAD_SIZE : (g + 1) * HEAD_SIZE].astype(f32)
        own = jnp.sum(q * nk, axis=-1, keepdims=True) * inverse_root
        m_c = m_g[g]
        top = jnp.maximum(m_c, own)
        a_c = jnp.exp(m_c - top)
        a_o = jnp.exp(own - top)
        inv = 1.0 / (l_g[g] * a_c + a_o)
        w_o = (a_o * inv).astype(bf16).astype(f32)
        ctx_ref[:, g * HEAD_SIZE : (g + 1) * HEAD_SIZE] = (
            acc_g[g] * (a_c * inv) + w_o * nv
        ).astype(bf16)
    sent(dsend, ret_sem)


def put_out(a_ref, b_ref, c_ref, a_out, b_out, c_out, sem):
    copies = [
        pltpu.make_async_copy(src, dst, sem.at[i])
        for i, (src, dst) in enumerate(((c_ref, c_out), (a_ref, a_out), (b_ref, b_out)))
    ]
    for c in copies:
        c.start()
    for c in copies:
        c.wait()


def shards(
    hidden_in,
    queries,
    cache_keys,
    cached_value_rows,
    cache_lengths,
    base_key_matrix,
    base_value_matrix,
    shrink_weights,
    pooled_up_weights,
    block_owner,
    block_slot,
):
    N, T = lax.axis_size("rep"), lax.axis_size("tp")
    R, D = hidden_in.shape
    C = cache_keys.shape[1]
    W = base_key_matrix.shape[1]
    G = queries.shape[1] // HEAD_SIZE
    ADP, _, RANK2 = shrink_weights.shape
    SL = CAP * BLK
    S = N * SL
    f32, bf16 = jnp.float32, jnp.bfloat16
    hbm = pl.BlockSpec(memory_space=pltpu.HBM)
    vmem = pl.BlockSpec(memory_space=pltpu.VMEM)
    dma = pltpu.SemaphoreType.DMA
    held = pl.pallas_call(
        functools.partial(kernel, N, T),
        out_shape=(
            jax.ShapeDtypeStruct((R, W), bf16),
            jax.ShapeDtypeStruct((R, W), bf16),
            jax.ShapeDtypeStruct((R, G * HEAD_SIZE), bf16),
        ),
        in_specs=[hbm] * 11,
        out_specs=(vmem, vmem, vmem),
        scratch_shapes=[
            pltpu.SMEM((R,), jnp.int32),
            pltpu.SMEM((R // BLK,), jnp.int32),
            pltpu.SMEM((R // BLK,), jnp.int32),
            pltpu.VMEM((R, D), bf16),
            pltpu.VMEM((R, G * HEAD_SIZE), bf16),
            pltpu.VMEM((R, C, W), bf16),
            pltpu.VMEM((R, C, W), bf16),
            pltpu.VMEM((T * D, 2 * W), bf16),
            pltpu.VMEM((D, ADP * RANK2), bf16),
            pltpu.VMEM((ADP * RANK2, 2 * W), bf16),
            pltpu.VMEM((T, R, D), bf16),
            pltpu.VMEM((N, SL, D + 128), bf16),
            pltpu.VMEM((N, SL, D + 128), bf16),
            pltpu.VMEM((T, S // T, RANK2), bf16),
            pltpu.VMEM((T, S // T, RANK2), bf16),
            pltpu.VMEM((S // T, RANK2), bf16),
            pltpu.VMEM((T, S // T, RANK2), bf16),
            pltpu.VMEM((N, SL, 2 * W), bf16),
            pltpu.VMEM((N, SL, 2 * W), bf16),
            pltpu.VMEM((R, G, HEAD_SIZE), f32),
            pltpu.VMEM((R, G, HEAD_SIZE), f32),
            pltpu.VMEM((R, G, HEAD_SIZE), f32),
            pltpu.VMEM((R, G, HEAD_SIZE), f32),
            pltpu.VMEM((R, 2 * W), f32),
            pltpu.VMEM((4, S // 4, 128), f32),
            pltpu.VMEM((G, R, HEAD_SIZE), f32),
            pltpu.VMEM((G, R, HEAD_SIZE), f32),
            pltpu.VMEM((G, R, HEAD_SIZE), f32),
            dma((7 + 3 * ADP,)),
            dma((2, KV_CHUNKS)),
            dma(()),
            dma((4,)),
            dma((2, T // 2, 2)),
            dma((2, T // 2, 2)),
            dma((2,)),
            dma(()),
            dma((4,)),
            dma((2,)),
        ],
        compiler_params=pltpu.CompilerParams(
            collective_id=0, has_side_effects=True, vmem_limit_bytes=VMEM_LIMIT
        ),
    )(
        *(
            pltpu.with_memory_space_constraint(x, pltpu.HBM)
            for x in (
                cache_lengths,
                block_owner[:, 0],
                block_slot,
                hidden_in,
                queries,
                cache_keys,
                cached_value_rows,
                base_key_matrix,
                base_value_matrix,
                shrink_weights,
                pooled_up_weights,
            )
        )
    )
    return pl.pallas_call(
        put_out,
        out_shape=tuple(jax.ShapeDtypeStruct(h.shape, h.dtype) for h in held),
        in_specs=[vmem] * 3,
        out_specs=(pl.BlockSpec(memory_space=pltpu.HBM),) * 3,
        scratch_shapes=[dma((3,))],
        compiler_params=pltpu.CompilerParams(vmem_limit_bytes=1024 * 1024),
    )(*held)


def solution(mesh):
    return jax.shard_map(
        shards,
        mesh=mesh,
        in_specs=(
            P("rep", "tp"),
            P("rep", "tp"),
            P("rep", None, "tp"),
            P("rep", None, "tp"),
            P("rep"),
            P(None, "tp"),
            P(None, "tp"),
            P("rep", "tp", None),
            P("rep", None, None, "tp"),
            P("rep", None),
            P("rep"),
        ),
        out_specs=(P("rep", "tp"), P("rep", "tp"), P("rep", "tp")),
        check_vma=False,
    )
```

```python
import functools
import jax
import jax.numpy as jnp
from jax import lax
from jax.experimental import pallas as pl
from jax.experimental.pallas import tpu as pltpu
from jax.sharding import PartitionSpec as P

HEAD_SIZE = 128
BLK = 4
CAP = 2
ADAPTER_SCALE = 0.5
MASKED = -1e30
MESH = pl.DeviceIdType.MESH
KV_CHUNKS = 6
VMEM_LIMIT = 40 * 1024 * 1024


def kernel(
    N,
    T,
    lens_hbm,
    owner_hbm,
    slot_hbm,
    hid_hbm,
    q_hbm,
    k_hbm,
    v_hbm,
    wk_hbm,
    wv_hbm,
    a_hbm,
    b_hbm,
    nk_ref,
    nv_ref,
    ctx_ref,
    lens_ref,
    owner_ref,
    slot_ref,
    hid,
    qin,
    kbuf,
    vbuf,
    wcat,
    acat,
    bcat,
    xbuf,
    sbuf,
    rbuf,
    part,
    prx,
    shr,
    srx,
    dsend,
    drx,
    qs,
    ms,
    ls,
    accs,
    base,
    hot,
    acc_g,
    m_g,
    l_g,
    load_sem,
    kv_sem,
    a2a_send,
    a2a_recv,
    ring_send,
    ring_recv,
    rs_sem,
    ag_send,
    ag_recv,
    ret_sem,
):
    f32, bf16 = jnp.float32, jnp.bfloat16
    R, D = hid.shape
    NB = R // BLK
    SL = CAP * BLK
    S = N * SL
    G = qin.shape[1] // HEAD_SIZE
    ADP = a_hbm.shape[0]
    RANK2 = a_hbm.shape[2]
    HALF = RANK2 // 2
    SG = S // T
    W = wk_hbm.shape[1]
    inverse_root = HEAD_SIZE ** (-0.5)
    me, z = lax.axis_index("rep"), lax.axis_index("tp")

    barrier = pltpu.get_barrier_semaphore()

    NC, NY = 2, 4
    NX = N // (NC * NY)
    mc, my, mx = lax.rem(me, NC), lax.rem(me // NC, NY), me // (NC * NY)
    xs = [lax.rem(mx + i, NX) * (NC * NY) for i in range(NX)]
    ys = [lax.rem(my + i, NY) * NC for i in range(NY)]
    cs = [mc, 1 - mc]
    far = lambda n: sorted(range(n), key=lambda i: -min(i, n - i))
    rep_peers = [
        xs[i] + ys[j] + cs[k]
        for i, j, k in sorted(
            ((i, j, k) for i in range(NX) for j in range(NY) for k in range(NC)),
            key=lambda t: -(min(t[0], NX - t[0]) + min(t[1], NY - t[1])),
        )
        if (i, j, k) != (0, 0, 0)
    ]
    tp_peers = [lax.rem(z + i, T) for i in far(T) if i]
    for p in tp_peers:
        pl.semaphore_signal(barrier, 1, device_id=(me, p), device_id_type=MESH)
    for p in rep_peers:
        pl.semaphore_signal(barrier, 1, device_id=(p, z), device_id_type=MESH)
    load_hid = pltpu.make_async_copy(hid_hbm, hid, load_sem.at[0])
    load_q = pltpu.make_async_copy(q_hbm, qin, load_sem.at[1])
    load_ids = [
        pltpu.make_async_copy(owner_hbm, owner_ref, load_sem.at[4 + 3 * ADP]),
        pltpu.make_async_copy(slot_hbm, slot_ref, load_sem.at[5 + 3 * ADP]),
        pltpu.make_async_copy(lens_hbm, lens_ref, load_sem.at[6 + 3 * ADP]),
    ]
    load_hid.start()
    for c in load_ids:
        c.start()
    load_q.start()
    load_a = [
        pltpu.make_async_copy(
            a_hbm.at[j], acat.at[:, pl.ds(j * RANK2, RANK2)], load_sem.at[2 + j]
        )
        for j in range(ADP)
    ]
    load_w = [
        pltpu.make_async_copy(wk_hbm, wcat.at[:, pl.ds(0, W)], load_sem.at[2 + ADP]),
        pltpu.make_async_copy(wv_hbm, wcat.at[:, pl.ds(W, W)], load_sem.at[3 + ADP]),
    ]
    bcat[...] = jnp.zeros_like(bcat)
    load_b = [
        pltpu.make_async_copy(
            b_hbm.at[j, i],
            bcat.at[pl.ds(j * RANK2 + i * HALF, HALF), pl.ds(i * W, W)],
            load_sem.at[4 + ADP + 2 * j + i],
        )
        for j in range(ADP)
        for i in range(2)
    ]
    RC = R // KV_CHUNKS
    load_kv = [
        [
            pltpu.make_async_copy(
                src.at[pl.ds(c * RC, RC)], dst.at[pl.ds(c * RC, RC)], kv_sem.at[i, c]
            )
            for i, (src, dst) in enumerate(((k_hbm, kbuf), (v_hbm, vbuf)))
        ]
        for c in range(KV_CHUNKS)
    ]
    for pair in load_kv:
        for c in pair:
            c.start()
    for c in load_a:
        c.start()
    for c in load_w:
        c.start()

    lane = lax.broadcasted_iota(jnp.int32, (1, R), 1)
    block_of = lane // BLK
    for c in load_ids:
        c.wait()
    owners = jnp.zeros((1, R), jnp.int32)
    slots = jnp.zeros((1, R), jnp.int32)
    for b in range(NB):
        owners = jnp.where(block_of == b, owner_ref[b], owners)
        slots = jnp.where(block_of == b, slot_ref[b], slots)
    ranks = jnp.zeros((1, R), jnp.int32)
    for b in range(NB):
        ranks = ranks + jnp.where((owners == owner_ref[b]) & (block_of > b), 1, 0)
    code = owners * SL + ranks * BLK + lane % BLK
    eye = lax.broadcasted_iota(jnp.int32, (R, R), 0) == lax.broadcasted_iota(jnp.int32, (R, R), 1)
    code_col = jnp.sum(jnp.where(eye, code.astype(f32), 0.0), axis=1, keepdims=True)
    slot_col = jnp.sum(jnp.where(eye, slots.astype(f32), 0.0), axis=1, keepdims=True)
    picks = (lax.broadcasted_iota(jnp.int32, (S, R), 0) == code).astype(bf16)
    one_hot = (
        lax.broadcasted_iota(jnp.int32, (R, 128), 1).astype(f32) == slot_col
    ).astype(bf16)
    load_hid.wait()
    sbuf[:, :, D:] = (
        jnp.dot(picks, one_hot, preferred_element_type=f32).reshape(N, SL, 128).astype(bf16)
    )
    for n in range(0, D, 256):
        sbuf[:, :, n : n + 256] = (
            jnp.dot(picks, hid[:, n : n + 256], preferred_element_type=f32)
            .reshape(N, SL, 256)
            .astype(bf16)
        )
    for c in load_b:
        c.start()

    def ring(direction, d, h, arriving):
        step = d if arriving else d - 1
        s = lax.rem(z + (T - step), T) if direction == 0 else lax.rem(z + step, T)
        to = lax.rem(z + 1, T) if direction == 0 else lax.rem(z + (T - 1), T)
        rows = pl.ds(h * (R // 2), R // 2)
        src = hid.at[rows] if d == 1 else xbuf.at[s, rows]
        return pltpu.make_async_remote_copy(
            src_ref=src,
            dst_ref=xbuf.at[s, rows],
            send_sem=ring_send.at[direction, d - 1, h],
            recv_sem=ring_recv.at[direction, d - 1, h],
            device_id=(me, to),
            device_id_type=MESH,
        )

    def carries(direction, d, h):
        return d < T // 2 or (d == T // 2 and h == direction)

    def to_rep(src, dst, sems, peer):
        return pltpu.make_async_remote_copy(
            src_ref=src,
            dst_ref=dst,
            send_sem=sems.at[0],
            recv_sem=sems.at[1],
            device_id=(peer, z),
            device_id_type=MESH,
        )

    def to_tp(src, dst, sems, peer):
        return pltpu.make_async_remote_copy(
            src_ref=src,
            dst_ref=dst,
            send_sem=sems.at[0],
            recv_sem=sems.at[1],
            device_id=(me, peer),
            device_id_type=MESH,
        )

    def arrived(buf, sems):
        pltpu.make_async_copy(buf, buf, sems.at[1]).wait()

    def sent(buf, sems):
        part_of = buf.at[pl.ds(0, buf.shape[0] - 1)]
        pltpu.make_async_copy(part_of, part_of, sems.at[0]).wait()

    def ring_event(d, h):
        for direction in range(2):
            if carries(direction, d, h):
                ring(direction, d, h, True).wait_recv()
                if carries(direction, d + 1, h):
                    ring(direction, d + 1, h, False).start()

    def base_block(s, first=False):
        x = hid[...] if first else xbuf[s]
        y = jnp.dot(
            x, wcat[pl.ds(pl.multiple_of(s * D, D), D), :], preferred_element_type=f32
        )
        base[...] = y if first else base[...] + y

    def attend(chunk):
        for c in load_kv[chunk]:
            c.wait()
        C = k_hbm.shape[1]
        rs = pl.ds(chunk * RC, RC)
        position = lax.broadcasted_iota(jnp.int32, (RC, G, C), 2)
        upto = jnp.stack(
            [jnp.full((G, C), lens_ref[chunk * RC + u], jnp.int32) for u in range(RC)]
        )
        s = lax.dot_general(
            qs[rs].astype(bf16),
            kbuf[rs],
            (((2,), (2,)), ((0,), (0,))),
            preferred_element_type=f32,
        )
        s = jnp.where(position < upto, s * inverse_root, MASKED)
        m = jnp.max(s, axis=-1, keepdims=True)
        p = jnp.exp(s - m)
        l = jnp.sum(p, axis=-1, keepdims=True)
        accs[rs] = lax.dot_general(
            p.astype(bf16),
            vbuf[rs],
            (((2,), (1,)), ((0,), (0,))),
            preferred_element_type=f32,
        )
        ms[rs] = jnp.broadcast_to(m, (RC, G, HEAD_SIZE))
        ls[rs] = jnp.broadcast_to(l, (RC, G, HEAD_SIZE))

    def forward_queries():
        load_q.wait()
        for g in range(G):
            qs[:, g, :] = qin[:, g * HEAD_SIZE : (g + 1) * HEAD_SIZE].astype(f32)

    pl.semaphore_wait(barrier, N - 1 + T - 1)
    for h in range(2):
        for direction in range(2):
            ring(direction, 1, h, False).start()
    for i in (0, 2, 1, 3):
        for j in (2, 1, 3, 0):
            for k in (1, 0):
                p = xs[i] + ys[j] + cs[k]
                if (i, j, k) == (0, 0, 0):
                    pltpu.make_async_copy(sbuf.at[p], rbuf.at[p], a2a_recv.at[0]).start()
                else:
                    pltpu.make_async_remote_copy(
                        src_ref=sbuf.at[p],
                        dst_ref=rbuf.at[me],
                        send_sem=a2a_send,
                        recv_sem=a2a_recv.at[i],
                        device_id=(p, z),
                        device_id_type=MESH,
                    ).start()
    forward_queries()
    for chunk in range(KV_CHUNKS):
        attend(chunk)
    for c in load_w:
        c.wait()
    base_block(z, True)
    for c in load_a:
        c.wait()
    NG = N // NX
    GR = NG * SL
    TG = T // NX
    def away(x):
        return lax.rem(mx + (NX - x), NX)

    def shrink(x):
        i = away(x)
        slabs = rbuf.at[pl.ds(x * NG, NG)]
        pltpu.make_async_copy(slabs, slabs, a2a_recv.at[i]).wait()
        rows = slabs[...].astype(f32).reshape(GR, D + 128)
        hot[x] = rows[:, D:]
        y = jnp.dot(rows[:, :D].astype(bf16), acat[...], preferred_element_type=f32)
        partial = jnp.zeros((GR, RANK2), f32)
        for j in range(ADP):
            partial = partial + y[:, j * RANK2 : (j + 1) * RANK2] * rows[:, D + j : D + j + 1]
        part[pl.ds(x * TG, TG)] = partial.reshape(TG, SG, RANK2).astype(part.dtype)
        for t in range(TG):
            to = x * TG + t

            @pl.when(to != z)
            def _():
                to_tp(part.at[to], prx.at[z], rs_sem, to).start()

            @pl.when(to == z)
            def _():
                pltpu.make_async_copy(part.at[to], prx.at[to], rs_sem.at[1]).start()

    def expand(x):
        i = away(x)
        slabs = srx.at[pl.ds(x * TG, TG)]
        pltpu.make_async_copy(slabs, slabs, ag_recv.at[i]).wait()
        shrunk = slabs[...].reshape(GR, RANK2)
        hots = hot[x]
        masked = jnp.concatenate(
            [shrunk * hots[:, j : j + 1].astype(bf16) for j in range(ADP)], axis=1
        )
        delta = ADAPTER_SCALE * jnp.dot(masked, bcat[...], preferred_element_type=f32)
        dsend[pl.ds(x * NG, NG)] = delta.reshape(NG, SL, 2 * W).astype(bf16)
        for y in (0, 1, 3, 2):
            for k in (1, 0):
                p = x * NG + y * NC + k

                @pl.when(p != me)
                def _():
                    to_rep(dsend.at[p], drx.at[me], ret_sem, p).start()

                @pl.when(p == me)
                def _():
                    pltpu.make_async_copy(dsend.at[p], drx.at[p], ret_sem.at[1]).start()

    ring_event(1, 0)
    ring_event(1, 1)
    for x in (0, 3, 1, 2):
        shrink(x)
    ring_event(2, 0)
    base_block(lax.rem(z + 1, T))
    base_block(lax.rem(z + T - 1, T))
    for src, dst in ((accs, acc_g), (ms, m_g), (ls, l_g)):
        for g in range(G):
            dst[g] = src[:, g, :]
    arrived(prx, rs_sem)
    total = prx[0].astype(f32)
    for t in range(1, T):
        total = total + prx[t].astype(f32)
    shr[...] = total.astype(bf16)
    mine = lax.rem(mx + (NX - z // TG), NX)
    for p in tp_peers:
        pltpu.make_async_remote_copy(
            src_ref=shr,
            dst_ref=srx.at[z],
            send_sem=ag_send,
            recv_sem=ag_recv.at[mine],
            device_id=(me, p),
            device_id_type=MESH,
        ).start()
    pltpu.make_async_copy(shr, srx.at[z], ag_recv.at[mine]).start()
    ring_event(2, 1)
    base_block(lax.rem(z + 2, T))
    base_block(lax.rem(z + T - 2, T))
    for c in load_b:
        c.wait()
    ring_event(3, 0)
    for x in (0, 3, 1, 2):
        expand(x)
    ring_event(3, 1)
    base_block(lax.rem(z + 3, T))
    base_block(lax.rem(z + T - 3, T))
    slabs = sbuf.at[pl.ds(0, N - 1)]
    pltpu.make_async_copy(slabs, slabs, a2a_send).wait()
    sent(part, rs_sem)
    slabs = srx.at[pl.ds(0, T - 1)]
    pltpu.make_async_copy(slabs, slabs, ag_send).wait()
    for h in range(2):
        ring_event(T // 2, h)
    base_block(lax.rem(z + T // 2, T))
    for h in range(2):
        for direction in range(2):
            for d in range(1, T // 2 + 1):
                if carries(direction, d, h):
                    ring(direction, d, h, False).wait_send()
    arrived(drx, ret_sem)

    spread = (
        lax.broadcasted_iota(jnp.int32, (R, S), 1).astype(f32) == code_col
    ).astype(bf16)
    got = drx[...].astype(f32).reshape(S, 2 * W).astype(bf16)
    fresh = (base[...] + jnp.dot(spread, got, preferred_element_type=f32)).astype(bf16)
    nk_ref[...] = fresh[:, :W]
    nv_ref[...] = fresh[:, W:]
    nk = fresh[:, :W].astype(f32)
    nv = fresh[:, W:].astype(f32)
    for g in range(G):
        q = qin[:, g * HEAD_SIZE : (g + 1) * HEAD_SIZE].astype(f32)
        own = jnp.sum(q * nk, axis=-1, keepdims=True) * inverse_root
        m_c = m_g[g]
        top = jnp.maximum(m_c, own)
        a_c = jnp.exp(m_c - top)
        a_o = jnp.exp(own - top)
        inv = 1.0 / (l_g[g] * a_c + a_o)
        w_o = (a_o * inv).astype(bf16).astype(f32)
        ctx_ref[:, g * HEAD_SIZE : (g + 1) * HEAD_SIZE] = (
            acc_g[g] * (a_c * inv) + w_o * nv
        ).astype(bf16)
    sent(dsend, ret_sem)


def put_out(a_ref, b_ref, c_ref, a_out, b_out, c_out, sem):
    copies = [
        pltpu.make_async_copy(src, dst, sem.at[i])
        for i, (src, dst) in enumerate(((c_ref, c_out), (a_ref, a_out), (b_ref, b_out)))
    ]
    for c in copies:
        c.start()
    for c in copies:
        c.wait()


def shards(
    hidden_in,
    queries,
    cache_keys,
    cached_value_rows,
    cache_lengths,
    base_key_matrix,
    base_value_matrix,
    shrink_weights,
    pooled_up_weights,
    block_owner,
    block_slot,
):
    N, T = lax.axis_size("rep"), lax.axis_size("tp")
    R, D = hidden_in.shape
    C = cache_keys.shape[1]
    W = base_key_matrix.shape[1]
    G = queries.shape[1] // HEAD_SIZE
    ADP, _, RANK2 = shrink_weights.shape
    SL = CAP * BLK
    S = N * SL
    f32, bf16 = jnp.float32, jnp.bfloat16
    hbm = pl.BlockSpec(memory_space=pltpu.HBM)
    vmem = pl.BlockSpec(memory_space=pltpu.VMEM)
    dma = pltpu.SemaphoreType.DMA
    held = pl.pallas_call(
        functools.partial(kernel, N, T),
        out_shape=(
            jax.ShapeDtypeStruct((R, W), bf16),
            jax.ShapeDtypeStruct((R, W), bf16),
            jax.ShapeDtypeStruct((R, G * HEAD_SIZE), bf16),
        ),
        in_specs=[hbm] * 11,
        out_specs=(vmem, vmem, vmem),
        scratch_shapes=[
            pltpu.SMEM((R,), jnp.int32),
            pltpu.SMEM((R // BLK,), jnp.int32),
            pltpu.SMEM((R // BLK,), jnp.int32),
            pltpu.VMEM((R, D), bf16),
            pltpu.VMEM((R, G * HEAD_SIZE), bf16),
            pltpu.VMEM((R, C, W), bf16),
            pltpu.VMEM((R, C, W), bf16),
            pltpu.VMEM((T * D, 2 * W), bf16),
            pltpu.VMEM((D, ADP * RANK2), bf16),
            pltpu.VMEM((ADP * RANK2, 2 * W), bf16),
            pltpu.VMEM((T, R, D), bf16),
            pltpu.VMEM((N, SL, D + 128), bf16),
            pltpu.VMEM((N, SL, D + 128), bf16),
            pltpu.VMEM((T, S // T, RANK2), bf16),
            pltpu.VMEM((T, S // T, RANK2), bf16),
            pltpu.VMEM((S // T, RANK2), bf16),
            pltpu.VMEM((T, S // T, RANK2), bf16),
            pltpu.VMEM((N, SL, 2 * W), bf16),
            pltpu.VMEM((N, SL, 2 * W), bf16),
            pltpu.VMEM((R, G, HEAD_SIZE), f32),
            pltpu.VMEM((R, G, HEAD_SIZE), f32),
            pltpu.VMEM((R, G, HEAD_SIZE), f32),
            pltpu.VMEM((R, G, HEAD_SIZE), f32),
            pltpu.VMEM((R, 2 * W), f32),
            pltpu.VMEM((4, S // 4, 128), f32),
            pltpu.VMEM((G, R, HEAD_SIZE), f32),
            pltpu.VMEM((G, R, HEAD_SIZE), f32),
            pltpu.VMEM((G, R, HEAD_SIZE), f32),
            dma((7 + 3 * ADP,)),
            dma((2, KV_CHUNKS)),
            dma(()),
            dma((4,)),
            dma((2, T // 2, 2)),
            dma((2, T // 2, 2)),
            dma((2,)),
            dma(()),
            dma((4,)),
            dma((2,)),
        ],
        compiler_params=pltpu.CompilerParams(
            collective_id=0, has_side_effects=True, vmem_limit_bytes=VMEM_LIMIT
        ),
    )(
        *(
            pltpu.with_memory_space_constraint(x, pltpu.HBM)
            for x in (
                cache_lengths,
                block_owner[:, 0],
                block_slot,
                hidden_in,
                queries,
                cache_keys,
                cached_value_rows,
                base_key_matrix,
                base_value_matrix,
                shrink_weights,
                pooled_up_weights,
            )
        )
    )
    return pl.pallas_call(
        put_out,
        out_shape=tuple(jax.ShapeDtypeStruct(h.shape, h.dtype) for h in held),
        in_specs=[vmem] * 3,
        out_specs=(pl.BlockSpec(memory_space=pltpu.HBM),) * 3,
        scratch_shapes=[dma((3,))],
        compiler_params=pltpu.CompilerParams(vmem_limit_bytes=1024 * 1024),
    )(*held)


def solution(mesh):
    return jax.shard_map(
        shards,
        mesh=mesh,
        in_specs=(
            P("rep", "tp"),
            P("rep", "tp"),
            P("rep", None, "tp"),
            P("rep", None, "tp"),
            P("rep"),
            P(None, "tp"),
            P(None, "tp"),
            P("rep", "tp", None),
            P("rep", None, None, "tp"),
            P("rep", None),
            P("rep"),
        ),
        out_specs=(P("rep", "tp"), P("rep", "tp"), P("rep", "tp")),
        check_vma=False,
    )
```
